32 devices in a mesh: replica: 16 (over z, y, x), shard: 2 (over core).
Axes of the slice: x: 2, y: 2, z: 4, core: 2. Of those that a mesh axis runs over, the one named last changes fastest.
Arguments:
- images: bfloat16 [16512, 1024], P(('replica', 'shard')), may hold values from -6 to 6
- cotangent: bfloat16 [16512, 1024], P(('replica', 'shard')), may hold values from -12 to 12
- qkv_weight: bfloat16 [1024, 3072], P('shard'), may hold values from -3 to 3
- proj_weight: bfloat16 [1024, 1024], P('shard'), may hold values from -0.5 to 0.5
- fc1_weight: bfloat16 [1024, 4096], P('shard'), may hold values from -0.1875 to 0.1875
- fc2_weight: bfloat16 [4096, 1024], P('shard'), may hold values from -0.09375 to 0.09375
- vectors: bfloat16 [10, 1024], P(None, 'shard'), may hold values from -1.5 to 2, as said below
- fc1_bias: bfloat16 [4096], P('shard'), may hold values from -3 to 3
Outputs:
- block_out: bfloat16 [16512, 1024], P(('replica', 'shard'))
- input_grad: float32 [16512, 1024], P(('replica', 'shard'))
- qkv_weight_grad: float32 [1024, 3072], P('shard')
- proj_weight_grad: float32 [1024, 1024], P('shard')
- fc1_weight_grad: float32 [1024, 4096], P('shard')
- fc2_weight_grad: float32 [4096, 1024], P('shard')
- vector_grads: float32 [10, 1024], P(None, 'shard')
- fc1_bias_grad: float32 [4096], P('shard')
The draws below stay inside these ranges and needn't reach their ends.
Inputs may be any that keep to these rules, and one draw needn't show every extreme that they name: `vectors`: gains and layer scales are positive.
All inputs are finite; a program needn't handle non-finite values.
Results may differ from the reference program's by a relative error of at most 0.0091.
Values may be sent and summed in bfloat16 or wider, within the bound.
No kernel may reach another device: no remote copies, remote signals or barrier semaphores. Data moves between devices by JAX's collectives and lax.ppermute only.
A program may use at most 320 MiB of HBM per device.

```python
import jax
import jax.numpy as jnp
from jax import lax

D = 1024
HEADS = 16
HEAD_DIM = 64
FF = 4096
IMG_DEV = 4
SEQ = 129
TOKENS = 16512


def draw_qkv_weight(key, part):
    base_key = jax.random.fold_in(key, 11)
    entries = jax.random.normal(base_key, (D, 3 * D), jnp.float32) * D ** (-0.5)
    return jnp.clip(entries, -3.0, 3.0).astype(jnp.bfloat16)


def draw_vectors(key, part):
    gain_key, bias_key, scale_key = jax.random.split(key, 3)
    row_id = jnp.arange(10)[:, None]
    is_gain = (row_id == 0) | (row_id == 6)
    is_scale = (row_id == 5) | (row_id == 9)
    gains = 1.0 + jnp.clip(0.25 * jax.random.normal(gain_key, (10, D), jnp.float32), -0.75, 0.75)
    biases = jnp.clip(0.4 * jax.random.normal(bias_key, (10, D), jnp.float32), -1.5, 1.5)
    scales = jnp.exp(jax.random.uniform(scale_key, (10, D), jnp.float32, -0.6931472, 0.6931472))
    return jnp.where(is_gain, gains, jnp.where(is_scale, scales, biases)).astype(jnp.bfloat16)


def strengthened(drawn, own_key, source, target, shards_of, factor):
    owner, partner = [(jnp.arange(drawn.shape[axis_at]) // (drawn.shape[axis_at] // shards_of)).reshape([-1 if axis == axis_at else 1 for axis in range(drawn.ndim)]) for axis_at in (source, target)]
    chosen = jax.random.permutation(own_key, shards_of)[partner]
    strong = (owner == chosen) | (owner == (partner + shards_of // 2) % shards_of)
    return jnp.where(strong, factor * drawn, drawn)


def levels(own_key, shape, cuts, least, high):
    factor_of, own = 1.0, jax.random.fold_in(own_key, 6)
    for dim, shards_of in cuts:
        steps = jnp.exp(jax.random.uniform(jax.random.fold_in(own, dim), (shards_of,), jnp.float32, least / len(cuts), high / len(cuts)))
        factor_of = factor_of * jnp.repeat(steps, shape[dim] // shards_of).reshape([-1 if axis == dim else 1 for axis in range(len(shape))])
    return factor_of


def gaussian(rng, shape, width, bound, shards=(), kind=jnp.bfloat16):
    level = levels(rng, shape, shards, -0.22, 0.18) if shards else 1.0
    drawn = jax.random.normal(rng, shape, jnp.float32) * width * level
    return jnp.minimum(jnp.maximum(drawn, -bound), bound).astype(kind)


def gaussian_with(rng, dims, scale, limit, cuts, heavy, held_as=jnp.bfloat16):
    result = scale * jax.random.normal(rng, dims, jnp.float32)
    if cuts:
        result = result * levels(rng, dims, cuts, -0.22, 0.18)
    return jnp.clip(strengthened(result, jax.random.fold_in(rng, 3), *heavy), -limit, limit).astype(held_as)


def setup_inputs(seed: int = 0) -> dict:
    arg_keys = jax.random.split(jax.random.key(seed), 9)
    images = gaussian(arg_keys[0], (TOKENS, D), 1.0, 6.0, ((0, 32),))
    cotangent = gaussian_with(arg_keys[1], (TOKENS, D), 1.0, 12.0, ((0, 32),), (0, 1, 32, 2.75))
    qkv_weight = draw_qkv_weight(jax.random.fold_in(arg_keys[8], 71), 0)
    proj_weight = gaussian(arg_keys[3], (D, D), (D // 8) ** -0.5, 0.5, ((0, 2),))
    fc1_weight = gaussian(arg_keys[4], (D, FF), D ** -0.5, 0.1875, ((0, 2),))
    fc2_weight = gaussian(arg_keys[5], (FF, D), FF ** -0.5, 0.09375, ((0, 2),))
    vectors = draw_vectors(jax.random.fold_in(arg_keys[8], 71), 0)
    fc1_bias = gaussian(arg_keys[7], (FF,), 0.5, 3.0, ((0, 2),))
    return {"images": images, "cotangent": cotangent, "qkv_weight": qkv_weight, "proj_weight": proj_weight, "fc1_weight": fc1_weight, "fc2_weight": fc2_weight, "vectors": vectors, "fc1_bias": fc1_bias}


EPS = 1e-06
PRECISE = lax.Precision.HIGHEST

@jax.custom_vjp
def low(v):
    return lax.optimization_barrier(v.astype(jnp.bfloat16)).astype(jnp.float32)

@jax.custom_vjp
def low_back(v):
    return v

def low_keep(v):
    return (low(v), None)

def low_pass(kept, grad):
    return (grad,)

def back_keep(v):
    return (v, None)

def back_low(kept, grad):
    return (low(grad),)
low.defvjp(low_keep, low_pass)
low_back.defvjp(back_keep, back_low)

def layer_norm(values_in, gain_row, shift_row):
    average = lax.optimization_barrier(jnp.mean(values_in, axis=-1, keepdims=True))
    centred = values_in - average
    variance = lax.optimization_barrier(jnp.mean(centred * centred, axis=-1, keepdims=True))
    return centred * lax.rsqrt(variance + EPS) * gain_row + shift_row

def block_forward(inputs, qkv_full, proj_full, fc1_full, fc2_full, vector_full, fc1_shift):
    gain_one, shift_one, bias_query, bias_value, bias_proj, scale_one, gain_two, shift_two, bias_two, scale_two = [vector_full[position] for position in range(10)]
    row_count = inputs.shape[0]
    image_count = row_count // SEQ
    normed = low(layer_norm(inputs, gain_one, shift_one))
    qkv_bias = jnp.concatenate([bias_query, jnp.zeros_like(bias_query), bias_value])
    packed = low(low_back(jnp.dot(normed, qkv_full, precision=PRECISE) + qkv_bias))
    packed = packed.reshape(image_count, SEQ, 3, HEADS, HEAD_DIM)
    queries = packed[:, :, 0]
    key_part = packed[:, :, 1]
    values = packed[:, :, 2]
    scores = low_back(jnp.einsum('nqhd,nkhd->nhqk', queries, key_part, precision=PRECISE) * HEAD_DIM ** (-0.5))
    weights = low(jax.nn.softmax(scores, axis=-1))
    attended = jnp.einsum('nhqk,nkhd->nqhd', weights, values, precision=PRECISE).reshape(row_count, D)
    attended = low(low_back(attended))
    branch_one = low_back(jnp.dot(attended, proj_full, precision=PRECISE) + bias_proj)
    middle = inputs + scale_one * branch_one
    normed_two = low(layer_norm(middle, gain_two, shift_two))
    hidden = low_back(jnp.dot(normed_two, fc1_full, precision=PRECISE) + fc1_shift)
    active = low(jax.nn.gelu(hidden, approximate=False))
    branch_two = low_back(jnp.dot(active, fc2_full, precision=PRECISE) + bias_two)
    return middle + scale_two * branch_two

def reference(images, cotangent, qkv_weight, proj_weight, fc1_weight, fc2_weight, vectors, fc1_bias):
    group_rows = IMG_DEV * SEQ

    def forward_all(inputs, qkv_full, proj_full, fc1_full, fc2_full, vector_full, fc1_shift):
        grouped = inputs.reshape(-1, group_rows, D)

        def one_group(piece_rows):
            return block_forward(piece_rows, qkv_full, proj_full, fc1_full, fc2_full, vector_full, fc1_shift)
        return lax.map(jax.checkpoint(one_group), grouped).reshape(-1, D)
    floats = (images.astype(jnp.float32), qkv_weight.astype(jnp.float32), proj_weight.astype(jnp.float32), fc1_weight.astype(jnp.float32), fc2_weight.astype(jnp.float32), vectors.astype(jnp.float32), fc1_bias.astype(jnp.float32))
    output, pullback = jax.vjp(forward_all, *floats)
    gradients = pullback(cotangent.astype(jnp.float32))
    return (output.astype(jnp.bfloat16), gradients[0], gradients[1], gradients[2], gradients[3], gradients[4], gradients[5], gradients[6])
```

```python
import jax
import jax.numpy as jnp
from jax import lax
from jax.experimental import pallas as pl
from jax.experimental.pallas import tpu as pltpu
from jax.sharding import PartitionSpec as P

HEADS = 16
HEAD_DIM = 64
SEQ = 129


EPS = 1e-06


def layer_norm(values_in, gain_row, shift_row):
    average = jnp.mean(values_in, axis=-1, keepdims=True)
    centred = values_in - average
    variance = jnp.mean(centred * centred, axis=-1, keepdims=True)
    return centred * lax.rsqrt(variance + EPS) * gain_row + shift_row


def gelu_exact(values_in):
    return jax.nn.gelu(values_in, approximate=False)


def outer_sum(left_side, right_side):
    return lax.dot_general(
        left_side, right_side, (((0,), (0,)), ((), ())), preferred_element_type=jnp.float32
    )


def back_product(left_side, right_side):
    return lax.dot_general(
        left_side, right_side, (((1,), (1,)), ((), ())), preferred_element_type=jnp.float32
    )


def swap_core(values):
    return lax.ppermute(values, "shard", [(0, 1), (1, 0)])


def pick(values, which, count, axis=0):
    return lax.dynamic_slice_in_dim(values, which * count, count, axis)


def partner(values, bit):
    size = lax.axis_size("replica")
    return lax.ppermute(values, "replica", [(i, i ^ (1 << bit)) for i in range(size)])


def orders(bits):
    main = list(range(bits - 1))
    return [main[turn:] + main[:turn] + [bits - 1] for turn in range(3)]


def halving(values, order):
    place = lax.axis_index("replica")
    for bit in order:
        own = (place >> bit) & 1
        count = values.shape[0] // 2
        arrived = partner(pick(values, 1 - own, count), bit)
        values = (
            pick(values, own, count).astype(jnp.float32) + arrived.astype(jnp.float32)
        ).astype(jnp.bfloat16)
    return values


def doubling(values, order):
    for bit in order[:0:-1]:
        values = jnp.concatenate([values, partner(values, bit)], axis=0)
    return values, partner(values, order[0])


def block_of(order):
    place = lax.axis_index("replica")
    number = 0
    for bit in order:
        number = number * 2 + ((place >> bit) & 1)
    return number


def settle_kernel(starts, blocks, own_ref, *refs):
    step = pl.program_id(0)
    out_ref = refs[-1]
    rows = out_ref.shape[0]
    for colour in range(3):
        near, far = refs[2 * colour], refs[2 * colour + 1]
        relative = jnp.bitwise_xor(step, own_ref[colour])
        lanes = slice(starts[colour], starts[colour + 1])

        @pl.when(relative < blocks // 2)
        def _():
            out_ref[:, lanes] = near[pl.ds(relative * rows, rows), :].astype(jnp.float32)

        @pl.when(relative >= blocks // 2)
        def _():
            out_ref[:, lanes] = far[pl.ds((relative - blocks // 2) * rows, rows), :].astype(
                jnp.float32
            )


def settle(pieces, starts, blocks):
    bits = blocks.bit_length() - 1
    owns = jnp.stack([block_of(order) for order in orders(bits)]).astype(jnp.int32)
    rows = pieces[0][0].shape[0] * 2
    flat = [part for piece in pieces for part in piece]
    return pl.pallas_call(
        lambda *refs: settle_kernel(starts, blocks, *refs),
        grid_spec=pltpu.PrefetchScalarGridSpec(
            num_scalar_prefetch=1,
            grid=(blocks,),
            in_specs=[pl.BlockSpec(part.shape, lambda i, own: (0, 0)) for part in flat],
            out_specs=pl.BlockSpec((rows // blocks, starts[-1]), lambda i, own: (i, 0)),
        ),
        out_shape=jax.ShapeDtypeStruct((rows, starts[-1]), jnp.float32),
        name="settle",
    )(owns, *flat)


def reduce_groups(values):
    blocks = lax.axis_size("replica")
    bits = blocks.bit_length() - 1
    width = values.shape[1]
    unit = width // 128
    first = -(-unit // 3)
    starts = (0, first * 128, min(2 * first, unit) * 128, width)
    pieces = []
    for colour, order in enumerate(orders(bits)):
        part = values[:, starts[colour] : starts[colour + 1]].astype(jnp.bfloat16)
        pieces.append(doubling(halving(part, order), order))
    return settle(pieces, starts, blocks)


def own_half(values, axis):
    core = lax.axis_index("shard")
    count = values.shape[axis] // 2
    arrived = swap_core(pick(values, 1 - core, count, axis).astype(jnp.bfloat16))
    return pick(values, core, count, axis) + arrived.astype(jnp.float32)


def shards(images, cotangent, qkv_weight, proj_weight, fc1_weight, fc2_weight, vectors, fc1_bias):
    gathered = (
        lax.all_gather(qkv_weight, "shard", axis=0, tiled=True),
        lax.all_gather(proj_weight, "shard", axis=0, tiled=True),
        lax.all_gather(fc1_weight, "shard", axis=0, tiled=True),
        lax.all_gather(fc2_weight, "shard", axis=0, tiled=True),
        lax.all_gather(vectors, "shard", axis=1, tiled=True),
        lax.all_gather(fc1_bias, "shard", axis=0, tiled=True),
    )
    qkv_full, proj_full, fc1_full, fc2_full, vector_full, bias_full = gathered
    vector_rows = vector_full.astype(jnp.float32)
    (
        gain_one,
        shift_one,
        bias_query,
        bias_value,
        bias_proj,
        scale_one,
        gain_two,
        shift_two,
        bias_two,
        scale_two,
    ) = [vector_rows[position] for position in range(10)]
    fc1_shift = bias_full.astype(jnp.float32)
    row_count = images.shape[0]
    width = images.shape[1]
    image_count = row_count // SEQ
    score_scale = HEAD_DIM ** (-0.5)
    inputs = images.astype(jnp.float32)
    normed_low = layer_norm(inputs, gain_one, shift_one).astype(jnp.bfloat16)
    qkv_bias = jnp.concatenate([bias_query, jnp.zeros_like(bias_query), bias_value])
    packed = (jnp.dot(normed_low, qkv_full, preferred_element_type=jnp.float32) + qkv_bias).astype(
        jnp.bfloat16
    )
    shaped = packed.reshape(image_count, SEQ, 3, HEADS, HEAD_DIM)
    queries = shaped[:, :, 0]
    key_part = shaped[:, :, 1]
    values = shaped[:, :, 2]
    scores = (
        jnp.einsum("nqhd,nkhd->nhqk", queries, key_part, preferred_element_type=jnp.float32)
        * score_scale
    )
    top_score = jnp.max(scores, axis=-1, keepdims=True)
    expo_scores = jnp.exp(scores - top_score)
    total_mass = jnp.sum(expo_scores, axis=-1, keepdims=True)
    probs = expo_scores / total_mass
    log_total = top_score + jnp.log(total_mass)
    attended = (
        jnp.einsum(
            "nhqk,nkhd->nqhd",
            probs.astype(jnp.bfloat16),
            values,
            preferred_element_type=jnp.float32,
        )
        .reshape(row_count, width)
        .astype(jnp.bfloat16)
    )
    branch_one = jnp.dot(attended, proj_full, preferred_element_type=jnp.float32) + bias_proj
    middle = inputs + scale_one * branch_one
    normed_two_low = layer_norm(middle, gain_two, shift_two).astype(jnp.bfloat16)
    hidden = jnp.dot(normed_two_low, fc1_full, preferred_element_type=jnp.float32) + fc1_shift
    active_low = gelu_exact(hidden).astype(jnp.bfloat16)
    branch_two = jnp.dot(active_low, fc2_full, preferred_element_type=jnp.float32) + bias_two
    block_out = (middle + scale_two * branch_two).astype(jnp.bfloat16)
    upstream = cotangent.astype(jnp.float32)
    grad_two = (upstream * scale_two).astype(jnp.bfloat16)
    grad_scale_two = jnp.sum(upstream * branch_two, axis=0)
    grad_bias_two = jnp.sum(grad_two.astype(jnp.float32), axis=0)
    grad_fc2 = outer_sum(active_low, grad_two)
    grad_active = back_product(grad_two, fc2_full)
    hidden_out, gelu_pull = jax.vjp(gelu_exact, hidden)
    grad_hidden = gelu_pull(grad_active)[0].astype(jnp.bfloat16)
    grad_fc1_bias = jnp.sum(grad_hidden.astype(jnp.float32), axis=0)
    grad_fc1 = outer_sum(normed_two_low, grad_hidden)
    grad_normed_two = back_product(grad_hidden, fc1_full)
    norm_out_two, norm_pull_two = jax.vjp(layer_norm, middle, gain_two, shift_two)
    grad_mid_part, grad_gain_two, grad_shift_two = norm_pull_two(grad_normed_two)
    grad_middle = upstream + grad_mid_part
    grad_one = (grad_middle * scale_one).astype(jnp.bfloat16)
    grad_scale_one = jnp.sum(grad_middle * branch_one, axis=0)
    grad_bias_proj = jnp.sum(grad_one.astype(jnp.float32), axis=0)
    grad_proj = outer_sum(attended, grad_one)
    grad_attended = (
        back_product(grad_one, proj_full)
        .astype(jnp.bfloat16)
        .reshape(image_count, SEQ, HEADS, HEAD_DIM)
    )
    scores_again = (
        jnp.einsum("nqhd,nkhd->nhqk", queries, key_part, preferred_element_type=jnp.float32)
        * score_scale
    )
    probs_again = jnp.exp(scores_again - log_total)
    grad_probs = jnp.einsum(
        "nqhd,nkhd->nhqk", grad_attended, values, preferred_element_type=jnp.float32
    )
    inner_sum = jnp.sum(grad_probs * probs_again, axis=-1, keepdims=True)
    grad_scores = (probs_again * (grad_probs - inner_sum)).astype(jnp.bfloat16)
    grad_queries = (
        jnp.einsum("nhqk,nkhd->nqhd", grad_scores, key_part, preferred_element_type=jnp.float32)
        * score_scale
    )
    grad_keys = (
        jnp.einsum("nhqk,nqhd->nkhd", grad_scores, queries, preferred_element_type=jnp.float32)
        * score_scale
    )
    grad_values = jnp.einsum(
        "nhqk,nqhd->nkhd",
        probs_again.astype(jnp.bfloat16),
        grad_attended,
        preferred_element_type=jnp.float32,
    )
    grad_packed = (
        jnp.stack([grad_queries, grad_keys, grad_values], axis=2)
        .reshape(row_count, 3 * width)
        .astype(jnp.bfloat16)
    )
    grad_packed_wide = grad_packed.astype(jnp.float32)
    grad_bias_query = jnp.sum(grad_packed_wide[:, :width], axis=0)
    grad_bias_value = jnp.sum(grad_packed_wide[:, 2 * width :], axis=0)
    grad_qkv = outer_sum(normed_low, grad_packed)
    grad_normed = back_product(grad_packed, qkv_full)
    norm_out_one, norm_pull_one = jax.vjp(layer_norm, inputs, gain_one, shift_one)
    grad_in_part, grad_gain_one, grad_shift_one = norm_pull_one(grad_normed)
    input_grad = grad_middle + grad_in_part
    vector_grad = jnp.stack(
        [
            grad_gain_one,
            grad_shift_one,
            grad_bias_query,
            grad_bias_value,
            grad_bias_proj,
            grad_scale_one,
            grad_gain_two,
            grad_shift_two,
            grad_bias_two,
            grad_scale_two,
        ]
    )
    core = lax.axis_index("shard")
    total_two = reduce_groups(own_half(grad_fc2, 0))
    total_one = reduce_groups(own_half(grad_fc1, 0))
    total_proj = reduce_groups(own_half(grad_proj, 0))
    total_qkv = reduce_groups(own_half(grad_qkv, 0))
    small = jnp.concatenate(
        [
            jnp.moveaxis(vector_grad.reshape(10, 2, 512), 1, 0).reshape(2, 5120),
            grad_fc1_bias.reshape(2, 2048),
        ],
        axis=1,
    ).reshape(2, 56, 128)
    small = small[core] + swap_core(small[1 - core])
    blocks = lax.axis_size("replica")
    for bit in range(blocks.bit_length() - 1):
        small = small + partner(small, bit)
    small = small.reshape(7168)
    return (
        block_out,
        input_grad,
        total_qkv,
        total_proj,
        total_one,
        total_two,
        small[:5120].reshape(10, 512),
        small[5120:],
    )


def solution(mesh):
    in_specs = (
        P(("replica", "shard"), None),
        P(("replica", "shard"), None),
        P("shard", None),
        P("shard", None),
        P("shard", None),
        P("shard", None),
        P(None, "shard"),
        P("shard"),
    )
    out_specs = (
        P(("replica", "shard"), None),
        P(("replica", "shard"), None),
        P("shard", None),
        P("shard", None),
        P("shard", None),
        P("shard", None),
        P(None, "shard"),
        P("shard"),
    )
    return jax.shard_map(shards, mesh=mesh, in_specs=in_specs, out_specs=out_specs, check_vma=False)
```

```python
import functools

import jax
import jax.numpy as jnp
from jax import lax
from jax.experimental import pallas as pl
from jax.experimental.pallas import tpu as pltpu
from jax.sharding import PartitionSpec as P

HEADS = 16
HEAD_DIM = 64
SEQ = 129
PAD = 144
EPS = 1e-06
F32 = jnp.float32
LOW = jnp.bfloat16


def dot(left, right):
    return lax.dot_general(left, right, (((1,), (0,)), ((), ())), preferred_element_type=F32)


def dot_back(left, right):
    return lax.dot_general(left, right, (((1,), (1,)), ((), ())), preferred_element_type=F32)


def dot_outer(left, right):
    return lax.dot_general(left, right, (((0,), (0,)), ((), ())), preferred_element_type=F32)


def call(body, core, ins, outs, grid=(1,), scratch=(), name=None):
    return pl.pallas_call(
        body,
        grid_spec=pltpu.PrefetchScalarGridSpec(
            num_scalar_prefetch=1,
            grid=grid,
            in_specs=[pl.BlockSpec(block, index) for _, block, index in ins],
            out_specs=[pl.BlockSpec(block, index) for _, _, block, index in outs],
            scratch_shapes=list(scratch),
        ),
        out_shape=[jax.ShapeDtypeStruct(shape, kind) for shape, kind, _, _ in outs],
        compiler_params=pltpu.CompilerParams(
            dimension_semantics=("arbitrary",) * len(grid), vmem_limit_bytes=56 * 1024 * 1024
        ),
        name=name,
    )(core, *[array for array, _, _ in ins])


def whole(array):
    zeros = (0,) * array.ndim
    return (array, array.shape, lambda *_: zeros)


def whole_out(shape, kind):
    zeros = (0,) * len(shape)
    return (shape, kind, shape, lambda *_: zeros)


def spread(rows_out, rows_in, first):
    place = lax.broadcasted_iota(jnp.int32, (rows_out, rows_in), 0) + first
    token = lax.broadcasted_iota(jnp.int32, (rows_out, rows_in), 1)
    return jnp.where(
        (place % PAD < SEQ) & (token == place // PAD * SEQ + place % PAD), 1.0, 0.0
    ).astype(LOW)


def gather_rows(rows_out, rows_in):
    token = lax.broadcasted_iota(jnp.int32, (rows_out, rows_in), 0)
    place = lax.broadcasted_iota(jnp.int32, (rows_out, rows_in), 1)
    return jnp.where(place == token // SEQ * PAD + token % SEQ, 1.0, 0.0).astype(LOW)


def halves(values, core, count):
    low, high = values[:, :count], values[:, count:]
    return jnp.where(core == 0, low, high), jnp.where(core == 0, high, low)


def joined(own, other, core):
    return jnp.concatenate(
        [jnp.where(core == 0, own, other), jnp.where(core == 0, other, own)], axis=1
    )


def norm_stats(values):
    centred = values - jnp.mean(values, axis=-1, keepdims=True)
    spread_rate = lax.rsqrt(jnp.mean(centred * centred, axis=-1, keepdims=True) + EPS)
    return centred * spread_rate, spread_rate


def norm_back(unit, rate, scaled):
    return rate * (
        scaled
        - jnp.mean(scaled, axis=-1, keepdims=True)
        - unit * jnp.mean(scaled * unit, axis=-1, keepdims=True)
    )


def colsum(values):
    return jnp.sum(values, axis=0, keepdims=True)


def enter_kernel(core_ref, images_ref, vec_ref, x_ref, own_ref, other_ref):
    step = pl.program_id(0)
    select = spread(PAD, images_ref.shape[0], step * PAD)
    x = dot(select, images_ref[...])
    x_ref[...] = x.astype(LOW)
    unit, _ = norm_stats(x)
    normed = (unit * vec_ref[0:1, :] + vec_ref[1:2, :]).astype(LOW)
    own_ref[...], other_ref[...] = halves(normed, core_ref[0], normed.shape[1] // 2)


def cotangent_kernel(core_ref, cot_ref, vec_ref, g_ref, ga_ref):
    step = pl.program_id(0)
    select = spread(PAD, cot_ref.shape[0], step * PAD)
    g = dot(select, cot_ref[...])
    g_ref[...] = g.astype(LOW)
    ga_ref[...] = (g * vec_ref[9:10, :]).astype(LOW)


def qkv_kernel(core_ref, own_ref, other_ref, w_own, w_other, bias_ref, out_ref):
    acc = dot(own_ref[...], w_own[...]) + dot(other_ref[...], w_other[...])
    out_ref[...] = (acc + bias_ref[...]).astype(LOW)


def lane_parts(values):
    lane = lax.broadcasted_iota(jnp.int32, values.shape, 1)
    zero = jnp.zeros_like(values)
    return jnp.where(lane < HEAD_DIM, values, zero), jnp.where(lane < HEAD_DIM, zero, values)


def pair_join(first, second):
    lane = lax.broadcasted_iota(jnp.int32, first.shape, 1)
    return jnp.where(lane < HEAD_DIM, first, second)


def masked_scores(q, k):
    scores = dot_back(q, k) * (HEAD_DIM**-0.5)
    key = lax.broadcasted_iota(jnp.int32, scores.shape, 1)
    return jnp.where(key < SEQ, scores, -1e30)


def attend_kernel(core_ref, q_ref, k_ref, v_ref, o_ref, lse_ref):
    for pair in range(q_ref.shape[1] // 128):
        lanes = slice(pair * 128, pair * 128 + 128)
        k, v = k_ref[:, lanes], v_ref[:, lanes]
        results, logs = [], []
        for q in lane_parts(q_ref[:, lanes]):
            scores = masked_scores(q, k)
            top = jnp.max(scores, axis=-1, keepdims=True)
            mass = jnp.exp(scores - top)
            total = jnp.sum(mass, axis=-1, keepdims=True)
            probs = (mass * (1.0 / total)).astype(LOW)
            results.append(dot(probs, v))
            logs.append(jnp.broadcast_to(top + jnp.log(total), results[-1].shape))
        o_ref[:, lanes] = pair_join(*results).astype(LOW)
        lse_ref[:, lanes] = pair_join(*logs)


def attend_back_kernel(core_ref, q_ref, k_ref, v_ref, lse_ref, go_ref, out_ref):
    width = go_ref.shape[1]
    group = pl.program_id(1)
    span = width * pl.num_programs(1)
    scale = HEAD_DIM**-0.5
    for pair in range(width // 128):
        lanes = slice(pair * 128, pair * 128 + 128)
        q, k, v, go = q_ref[:, lanes], k_ref[:, lanes], v_ref[:, lanes], go_ref[:, lanes]
        lse = lse_ref[:, lanes]
        parts = []
        for head, (q_part, go_part) in enumerate(zip(lane_parts(q), lane_parts(go))):
            column = head * HEAD_DIM
            probs = jnp.exp(masked_scores(q_part, k) - lse[:, column : column + 1])
            grad_probs = dot_back(go_part, v)
            inner = jnp.sum(grad_probs * probs, axis=-1, keepdims=True)
            grad_scores = (probs * (grad_probs - inner)).astype(LOW)
            parts.append(
                (
                    dot(grad_scores, k) * scale,
                    dot_outer(grad_scores, q) * scale,
                    dot_outer(probs.astype(LOW), go),
                )
            )
        for block in range(3):
            start = pl.multiple_of(block * span + group * width + pair * 128, 128)
            out_ref[:, pl.ds(start, 128)] = pair_join(parts[0][block], parts[1][block]).astype(LOW)


def project_kernel(core_ref, o_ref, w_own, w_other, x_ref, vec_ref, h_ref, a_ref, own_ref, other_ref, o_other_ref):
    core = core_ref[0]
    count = o_ref.shape[1] // 2
    o_own, o_other = halves(o_ref[...], core, count)
    o_other_ref[...] = o_other
    branch = dot(o_own, w_own[...]) + dot(o_other, w_other[...]) + vec_ref[4:5, :]
    a_ref[...] = branch.astype(LOW)
    middle = x_ref[...].astype(F32) + vec_ref[5:6, :] * branch
    h_ref[...] = middle
    unit, _ = norm_stats(middle)
    normed = (unit * vec_ref[6:7, :] + vec_ref[7:8, :]).astype(LOW)
    own_ref[...], other_ref[...] = halves(normed, core, count)


def hidden_kernel(core_ref, own_ref, other_ref, w_own, w_other, bias_ref, u_ref, d_ref):
    z = dot(own_ref[...], w_own[...]) + dot(other_ref[...], w_other[...]) + bias_ref[...]
    phi = 0.5 + 0.5 * lax.erf(z * 0.7071067811865476)
    u_ref[...] = (z * phi).astype(LOW)
    d_ref[...] = (phi + z * (jnp.exp(-0.5 * (z * z)) * 0.3989422804014327)).astype(LOW)


def middle_kernel(
    core_ref,
    ga_ref,
    u_own,
    u_other,
    d_own,
    d_other,
    w2_own,
    w2_other,
    w1_own,
    w1_other,
    h_ref,
    a_ref,
    g_ref,
    vec_ref,
    gz_ref,
    gzb_ref,
    out_ref,
    gh_ref,
    ga1_ref,
    sums_ref,
    acc_two,
    acc_own,
    acc_other,
):
    step = pl.program_id(0)
    core = core_ref[0]
    mine = step < pl.num_programs(0) // 2
    u = jnp.where(mine, u_own[...], u_other[...])
    d = jnp.where(mine, d_own[...], d_other[...])
    w2 = jnp.where(mine, w2_own[...], w2_other[...])
    gz32 = dot_back(ga_ref[...], w2) * d.astype(F32)
    gz = gz32.astype(LOW)
    gz_ref[...] = gz
    gzb_ref[...] = colsum(gz.astype(F32))

    @pl.when(step == 0)
    def _():
        acc_two[...] = jnp.zeros_like(acc_two)
        acc_own[...] = jnp.zeros_like(acc_own)
        acc_other[...] = jnp.zeros_like(acc_other)

    acc_two[...] += dot(u, w2)
    acc_own[...] += dot_back(gz, w1_own[...])
    acc_other[...] += dot_back(gz, w1_other[...])

    @pl.when(step == pl.num_programs(0) - 1)
    def _():
        h = h_ref[...]
        g = g_ref[...].astype(F32)
        branch = acc_two[...] + vec_ref[8:9, :]
        result = (h + vec_ref[9:10, :] * branch).astype(LOW)
        out_ref[...] = dot(gather_rows(out_ref.shape[0], h.shape[0]), result).astype(LOW)
        unit, rate = norm_stats(h)
        grad = joined(acc_own[...], acc_other[...], core)
        gh = g + norm_back(unit, rate, grad * vec_ref[6:7, :])
        gh_ref[...] = gh
        ga1 = (gh * vec_ref[5:6, :]).astype(LOW)
        ga1_ref[...] = ga1
        sums_ref[0:1, :] = colsum(ga1.astype(F32))
        sums_ref[1:2, :] = colsum(gh * a_ref[...].astype(F32))
        sums_ref[2:3, :] = colsum(grad * unit)
        sums_ref[3:4, :] = colsum(grad)
        sums_ref[4:5, :] = colsum(ga_ref[...].astype(F32))
        sums_ref[5:6, :] = colsum(g * branch)
        sums_ref[6:8, :] = jnp.zeros_like(sums_ref[6:8, :])


def project_back_kernel(core_ref, ga_ref, w_own, w_other, go_ref):
    ga = ga_ref[...]
    go_ref[...] = joined(dot_back(ga, w_own[...]), dot_back(ga, w_other[...]), core_ref[0]).astype(LOW)


def leave_kernel(core_ref, dq_ref, w_own, w_other, x_ref, gh_ref, vec_ref, out_ref, bias_ref, sums_ref, acc_own, acc_other):
    step = pl.program_id(0)
    grad_in = dq_ref[...]

    @pl.when(step == 0)
    def _():
        acc_own[...] = jnp.zeros_like(acc_own)
        acc_other[...] = jnp.zeros_like(acc_other)

    acc_own[...] += dot_back(grad_in, w_own[...])
    acc_other[...] += dot_back(grad_in, w_other[...])
    bias_ref[...] = colsum(grad_in.astype(F32))

    @pl.when(step == pl.num_programs(0) - 1)
    def _():
        unit, rate = norm_stats(x_ref[...].astype(F32))
        grad = joined(acc_own[...], acc_other[...], core_ref[0])
        sums_ref[0:1, :] = colsum(grad * unit)
        sums_ref[1:2, :] = colsum(grad)
        sums_ref[2:8, :] = jnp.zeros_like(sums_ref[2:8, :])
        result = gh_ref[...] + norm_back(unit, rate, grad * vec_ref[0:1, :])
        for image in range(result.shape[0] // PAD):
            out_ref[image * SEQ : image * SEQ + SEQ, :] = result[image * PAD : image * PAD + SEQ, :]


def store_blocks(place, values, first, lanes, send_ref, keep_ref, rows):
    count = keep_ref.shape[0] // rows
    for index in range(values.shape[0] // rows):
        relative = jnp.bitwise_xor(first + index, place)
        part = values[index * rows : index * rows + rows, :]

        @pl.when(relative < count)
        def _():
            keep_ref[pl.ds(pl.multiple_of(relative * rows, rows), rows), lanes] = part

        @pl.when(relative >= count)
        def _():
            send_ref[pl.ds(pl.multiple_of((relative - count) * rows, rows), rows), lanes] = part


def weight_kernel(info_ref, *refs, rows, pairs, tile, extra):
    send_ref, keep_ref = refs[-2:]
    at = pl.program_id(0)
    base = 0
    for number, tiles in enumerate(pairs):
        x_own, x_far, y_own, y_far = refs[4 * number : 4 * number + 4]

        @pl.when((at >= base) & (at < base + tiles))
        def _():
            acc = dot_outer(x_own[...], y_own[...]) + dot_outer(x_far[...], y_far[...])
            lanes = pl.ds(pl.multiple_of(at * tile, 128), tile)
            store_blocks(info_ref[1], acc.astype(LOW), 0, lanes, send_ref, keep_ref, rows)

        base += tiles
    if extra:
        extra_ref = refs[4 * len(pairs)]

        @pl.when(at == 0)
        def _():
            lanes = slice(base * tile, base * tile + 128)
            store_blocks(info_ref[1], extra_ref[...].astype(LOW), 0, lanes, send_ref, keep_ref, rows)


def weight_grad(info, blocks, pairs, tile, extra=None, name=None):
    ins = []
    counts = []
    base = 0
    rows = None
    for x_own, x_far, y_own, y_far, first, tiles, halved in pairs:
        rows = x_far.shape[1]
        counts.append(tiles)

        def column(i, *_, base=base, first=first, tiles=tiles):
            return (0, first + jnp.clip(i - base, 0, tiles - 1))

        own_index = (lambda i, info: (0, info[0])) if halved else (lambda i, info: (0, 0))
        ins += [
            (x_own, (x_own.shape[0], rows), own_index),
            whole(x_far),
            (y_own, (y_own.shape[0], tile), column),
            (y_far, (y_far.shape[0], tile), column),
        ]
        base += tiles
    width = base * tile
    if extra is not None:
        ins.append(whole(extra))
        width += 128
    body = functools.partial(
        weight_kernel, rows=rows // blocks, pairs=counts, tile=tile, extra=extra is not None
    )
    shape = (rows // 2, width)
    return call(body, info, ins, [whole_out(shape, LOW)] * 2, grid=(base,), name=name)


def tall_kernel(info_ref, x_own, x_far, y_own, y_far, send_ref, keep_ref, *, rows):
    at = pl.program_id(0)
    acc = dot_outer(x_own[...], y_own[...]) + dot_outer(x_far[...], y_far[...])
    first = at * (acc.shape[0] // rows)
    store_blocks(info_ref[1], acc.astype(LOW), first, slice(None), send_ref, keep_ref, rows)


def tall_grad(info, blocks, x_own, x_far, y_own, y_far, column, width, name=None):
    total = x_own.shape[1]
    tile = 512
    y_index = lambda i, *_: (0, column)
    ins = [
        (x_own, (x_own.shape[0], tile), lambda i, *_: (0, i)),
        (x_far, (x_far.shape[0], tile), lambda i, *_: (0, i)),
        (y_own, (y_own.shape[0], width), y_index),
        (y_far, (y_far.shape[0], width), y_index),
    ]
    body = functools.partial(tall_kernel, rows=total // blocks)
    shape = (total // 2, width)
    return call(body, info, ins, [whole_out(shape, LOW)] * 2, grid=(total // tile,), name=name)


def settle_kernel(info_ref, *refs, plan, blocks):
    step = pl.program_id(0)
    inputs, outputs = refs[: 2 * len(plan)], refs[2 * len(plan) :]
    for colour, moves in enumerate(plan):
        near, far = inputs[2 * colour], inputs[2 * colour + 1]
        relative = jnp.bitwise_xor(step, info_ref[1 + colour])
        for start, stop, number, lane in moves:
            out_ref = outputs[number]
            rows = out_ref.shape[0]
            lanes = slice(lane, lane + stop - start)

            @pl.when(relative < blocks // 2)
            def _():
                at = pl.multiple_of(relative * rows, rows)
                out_ref[:, lanes] = near[pl.ds(at, rows), start:stop].astype(F32)

            @pl.when(relative >= blocks // 2)
            def _():
                at = pl.multiple_of((relative - blocks // 2) * rows, rows)
                out_ref[:, lanes] = far[pl.ds(at, rows), start:stop].astype(F32)


def settle(info, blocks, pieces, plan, widths, name=None):
    rows = pieces[0][0].shape[0] * 2
    flat = [whole(part) for piece in pieces for part in piece]
    outs = [
        ((rows, width), F32, (rows // blocks, width), lambda i, *_: (i, 0)) for width in widths
    ]
    body = functools.partial(settle_kernel, plan=plan, blocks=blocks)
    return call(body, info, flat, outs, grid=(blocks,), name=name)


def swap_core(values):
    return lax.ppermute(values, "shard", [(0, 1), (1, 0)])


def partner(values, bit):
    size = lax.axis_size("replica")
    return lax.ppermute(values, "replica", [(i, i ^ (1 << bit)) for i in range(size)])


def orders():
    bits = lax.axis_size("replica").bit_length() - 1
    rest = list(range(3, bits - 1))
    return [[0, 2, 1] + rest + [bits - 1], [1, 2, 0] + rest + [bits - 1]]


def block_place(order):
    place = lax.axis_index("replica")
    number = 0
    for bit in order[:-1]:
        number = number * 2 + ((place >> bit) & 1)
    return number


def added(left, right):
    return (left.astype(F32) + right.astype(F32)).astype(LOW)


def reduce_colour(send, keep, order):
    for position, bit in enumerate(order[:-1]):
        total = added(keep, partner(send, bit))
        if position < len(order) - 2:
            count = total.shape[0] // 2
            send, keep = total[count:], total[:count]
    total = added(total, partner(total, order[-1]))
    for bit in order[-2:0:-1]:
        total = jnp.concatenate([total, partner(total, bit)], axis=0)
    return total, partner(total, order[0])


def shards(images, cotangent, qkv_weight, proj_weight, fc1_weight, fc2_weight, vectors, fc1_bias):
    count, width = images.shape
    half = width // 2
    imgs = count // SEQ
    rows = imgs * PAD
    hidden = fc1_weight.shape[1]
    hid_half = hidden // 2
    core = lax.axis_index("shard")
    core_info = core.astype(jnp.int32).reshape(1)
    both = orders()
    blocks = lax.axis_size("replica") // 2
    places = [block_place(order) for order in both]
    infos = [jnp.stack([core, place]).astype(jnp.int32) for place in places]
    settle_info = jnp.stack([core, places[0], places[1]]).astype(jnp.int32)

    small_own = jnp.concatenate([vectors, fc1_bias.reshape(-1, half)], axis=0)
    small_far = swap_core(small_own)
    qkv_far = swap_core(qkv_weight)
    proj_far = swap_core(proj_weight)
    fc1_far = swap_core(fc1_weight)
    fc2_far = swap_core(fc2_weight)

    own32, far32 = small_own.astype(F32), small_far.astype(F32)
    first = jnp.where(core == 0, own32, far32)
    second = jnp.where(core == 0, far32, own32)
    vec = jnp.concatenate([first[:10], second[:10]], axis=1)
    qkv_bias = jnp.concatenate([vec[2:3], jnp.zeros_like(vec[2:3]), vec[3:4]], axis=1)
    hid_bias = jnp.concatenate([first[10:].reshape(1, hid_half), second[10:].reshape(1, hid_half)], axis=1)

    by_image = lambda i, *_: (i, 0)
    x, n1_own, n1_other = call(
        enter_kernel,
        core_info,
        [whole(images), whole(vec)],
        [
            ((rows, width), LOW, (PAD, width), by_image),
            ((rows, half), LOW, (PAD, half), by_image),
            ((rows, half), LOW, (PAD, half), by_image),
        ],
        grid=(imgs,),
        name="enter",
    )
    tile = 512
    column = lambda i, *_: (0, i)
    (qkv,) = call(
        qkv_kernel,
        core_info,
        [
            whole(n1_own),
            whole(n1_other),
            (qkv_weight, (half, tile), column),
            (qkv_far, (half, tile), column),
            (qkv_bias, (1, tile), column),
        ],
        [((rows, 3 * width), LOW, (rows, tile), column)],
        grid=(3 * width // tile,),
        name="qkv",
    )
    group = 256
    groups = width // group
    part = lambda block: (qkv, (PAD, group), lambda i, j, *_: (i, block * groups + j))
    head_index = lambda i, j, *_: (i, j)
    o, lse = call(
        attend_kernel,
        core_info,
        [part(0), part(1), part(2)],
        [
            ((rows, width), LOW, (PAD, group), head_index),
            ((rows, width), F32, (PAD, group), head_index),
        ],
        grid=(imgs, groups),
        name="attend",
    )
    h, a1, n2_own, n2_other, o_other = call(
        project_kernel,
        core_info,
        [whole(o), whole(proj_weight), whole(proj_far), whole(x), whole(vec)],
        [
            whole_out((rows, width), F32),
            whole_out((rows, width), LOW),
            whole_out((rows, half), LOW),
            whole_out((rows, half), LOW),
            whole_out((rows, half), LOW),
        ],
        name="project",
    )
    tiles = hid_half // tile

    def hidden_half(mine):
        def at(i, info):
            side = info[0] if mine else 1 - info[0]
            return (0, side * tiles + i)

        return call(
            hidden_kernel,
            core_info,
            [
                whole(n2_own),
                whole(n2_other),
                (fc1_weight, (half, tile), at),
                (fc1_far, (half, tile), at),
                (hid_bias, (1, tile), at),
            ],
            [
                ((rows, hid_half), LOW, (rows, tile), column),
                ((rows, hid_half), LOW, (rows, tile), column),
            ],
            grid=(tiles,),
            name="hidden",
        )

    u_other, d_other = hidden_half(False)
    u_far = swap_core(u_other)
    u_own, d_own = hidden_half(True)

    g, ga2 = call(
        cotangent_kernel,
        core_info,
        [whole(cotangent), whole(vec)],
        [
            ((rows, width), LOW, (PAD, width), by_image),
            ((rows, width), LOW, (PAD, width), by_image),
        ],
        grid=(imgs,),
        name="cotangent",
    )
    ga2_far = swap_core(ga2)

    parts_two = [
        tall_grad(infos[c], blocks, u_own, u_far, ga2, ga2_far, c, half, name="grad_fc2")
        for c in range(2)
    ]
    reduced_two = [reduce_colour(*parts_two[c], both[c]) for c in range(2)]

    last = 2 * tiles
    own_col = lambda i, *_: (0, jnp.minimum(i, tiles - 1))
    far_col = lambda i, *_: (0, jnp.maximum(i - tiles, 0))
    own_row = lambda i, *_: (jnp.minimum(i, tiles - 1), 0)
    far_row = lambda i, *_: (jnp.maximum(i - tiles, 0), 0)
    turn = lambda i, info: (0, (info[0] * tiles + i) % last)
    gz, gz_bias, block_out, gh, ga1, mid_sums = call(
        middle_kernel,
        core_info,
        [
            whole(ga2),
            (u_own, (rows, tile), own_col),
            (u_other, (rows, tile), far_col),
            (d_own, (rows, tile), own_col),
            (d_other, (rows, tile), far_col),
            (fc2_weight, (tile, width), own_row),
            (fc2_far, (tile, width), far_row),
            (fc1_weight, (half, tile), turn),
            (fc1_far, (half, tile), turn),
            whole(h),
            whole(a1),
            whole(g),
            whole(vec),
        ],
        [
            ((rows, hidden), LOW, (rows, tile), turn),
            ((1, hidden), F32, (1, tile), turn),
            whole_out((count, width), LOW),
            whole_out((rows, width), F32),
            whole_out((rows, width), LOW),
            whole_out((8, width), F32),
        ],
        grid=(last,),
        scratch=[
            pltpu.VMEM((rows, width), F32),
            pltpu.VMEM((rows, half), F32),
            pltpu.VMEM((rows, half), F32),
        ],
        name="middle",
    )
    gz_far = swap_core(gz)
    n2_far = swap_core(n2_other)
    ga1_far = swap_core(ga1)
    o_far = swap_core(o_other)
    n1_far = swap_core(n1_other)

    (go,) = call(
        project_back_kernel,
        core_info,
        [whole(ga1), whole(proj_weight), whole(proj_far)],
        [whole_out((rows, width), LOW)],
        name="project_back",
    )

    wide = hidden // 2 // tile
    parts_one = [
        weight_grad(
            infos[c], blocks, [(n2_own, n2_far, gz, gz_far, c * wide, wide, False)], tile, name="grad_fc1"
        )
        for c in range(2)
    ]
    reduced_one = [reduce_colour(*parts_one[c], both[c]) for c in range(2)]

    (dqkv,) = call(
        attend_back_kernel,
        core_info,
        [
            part(0),
            part(1),
            part(2),
            (lse, (PAD, group), head_index),
            (go, (PAD, group), head_index),
        ],
        [((rows, 3 * width), LOW, (PAD, 3 * width), lambda i, j, *_: (i, 0))],
        grid=(imgs, groups),
        name="attend_back",
    )
    dqkv_far = swap_core(dqkv)
    input_grad, qkv_bias_sums, end_sums = call(
        leave_kernel,
        core_info,
        [
            (dqkv, (rows, tile), column),
            (qkv_weight, (half, tile), column),
            (qkv_far, (half, tile), column),
            whole(x),
            whole(gh),
            whole(vec),
        ],
        [
            whole_out((count, width), F32),
            ((1, 3 * width), F32, (1, tile), column),
            whole_out((8, width), F32),
        ],
        grid=(3 * width // tile,),
        scratch=[pltpu.VMEM((rows, half), F32), pltpu.VMEM((rows, half), F32)],
        name="leave",
    )
    vector_sums = jnp.concatenate(
        [
            end_sums[0:2],
            qkv_bias_sums[:, :width],
            qkv_bias_sums[:, 2 * width :],
            mid_sums[0:6],
        ],
        axis=0,
    )
    small = jnp.concatenate(
        [
            jnp.swapaxes(vector_sums.reshape(10, 2, half), 0, 1).reshape(2, -1),
            gz_bias.reshape(2, hid_half),
        ],
        axis=1,
    ).reshape(2, -1, 128)
    small = small[core] + swap_core(small[1 - core])
    used = small.shape[0]
    small = jnp.concatenate([small, jnp.zeros((half - used, 128), F32)], axis=0)

    cut = width * 2 // tile
    parts_in = [
        weight_grad(
            infos[0], blocks, [(n1_own, n1_far, dqkv, dqkv_far, 0, cut, False)], tile, name="grad_qkv"
        ),
        weight_grad(
            infos[1],
            blocks,
            [
                (n1_own, n1_far, dqkv, dqkv_far, cut, width // tile, False),
                (o, o_far, ga1, ga1_far, 0, width // tile, True),
            ],
            tile,
            extra=small,
            name="grad_qkv_proj",
        ),
    ]
    reduced_in = [reduce_colour(*parts_in[c], both[c]) for c in range(2)]

    (total_two,) = settle(
        settle_info, blocks, reduced_two, [[(0, half, 0, 0)], [(0, half, 0, half)]], [width], name="settle_fc2"
    )
    (total_one,) = settle(
        settle_info,
        blocks,
        reduced_one,
        [[(0, hid_half, 0, 0)], [(0, hid_half, 0, hid_half)]],
        [hidden],
        name="settle_fc1",
    )
    total_qkv, total_proj, total_small = settle(
        settle_info,
        blocks,
        reduced_in,
        [
            [(0, 2 * width, 0, 0)],
            [(0, width, 0, 2 * width), (width, 2 * width, 1, 0), (2 * width, 2 * width + 128, 2, 0)],
        ],
        [3 * width, width, 128],
        name="settle_in",
    )
    total_small = total_small[:used].reshape(-1)
    return (
        block_out,
        input_grad,
        total_qkv,
        total_proj,
        total_one,
        total_two,
        total_small[: 10 * half].reshape(10, half),
        total_small[10 * half :],
    )


def solution(mesh):
    in_specs = (
        P(("replica", "shard"), None),
        P(("replica", "shard"), None),
        P("shard", None),
        P("shard", None),
        P("shard", None),
        P("shard", None),
        P(None, "shard"),
        P("shard"),
    )
    out_specs = (
        P(("replica", "shard"), None),
        P(("replica", "shard"), None),
        P("shard", None),
        P("shard", None),
        P("shard", None),
        P("shard", None),
        P(None, "shard"),
        P("shard"),
    )
    return jax.shard_map(shards, mesh=mesh, in_specs=in_specs, out_specs=out_specs, check_vma=False)
```
